128 devices in a mesh: rep: 4 (over y), set: 32 (over z, x, core).
Axes of the slice: x: 4, y: 4, z: 4, core: 2. Of those that a mesh axis runs over, the one named last changes fastest.
Arguments:
- scenarios: bfloat16 [3, 8192, 20000], P(None, ('rep', 'set')), may hold values from -6 to 6
- projection: bfloat16 [20000, 256], replicated, may hold values from -0.0390625 to 0.0390625
- coefs: bfloat16 [3, 256, 1024, 64], P(None, None, 'set'), may hold values from -0.0234375 to 0.0234375
- exercise: float32 [3, 1024, 64], P(None, 'set'), may hold values from -0.2 to 0
- block_set: int32 [1024], P('set'), may hold values from 0 to 127, as said below
- block_live: int32 [1024], P('set'), may hold values from 1 to 64
Outputs:
- exposure: float32 [3, 128], P(None, 'set')
- spread: float32 [3, 128], P(None, 'set')
The draws below stay inside these ranges and needn't reach their ends.
Inputs may be any that keep to these rules, and one draw needn't show every extreme that they name: `block_set`: every netting set owns at least one block.
All inputs are finite; a program needn't handle non-finite values.
Results may differ from the reference program's by a relative error of at most 0.0011.
Values may be sent and summed in bfloat16 or wider, within the bound.
No kernel may reach another device: no remote copies, remote signals or barrier semaphores. Data moves between devices by JAX's collectives and lax.ppermute only.
A program may use at most 128 MiB of HBM per device.

```python
import math
import jax
import jax.numpy as jnp
from jax import lax

FACT = 20000
BASIS = 256
TB = 64
STEPS = 3
PATHS = 1024
BPD = 32
SPD = 4
REPL = 8
ROWS = 8192
NSETS = 128
NBLK = 1024


def draw_block_set(key, part):
    first_key, second_key, order_key = jax.random.split(key, 3)
    first = jax.random.randint(first_key, (NBLK - NSETS,), 0, NSETS)
    second = jax.random.randint(second_key, (NBLK - NSETS,), 0, NSETS)
    extra = jnp.minimum(first, second).astype(jnp.int32)
    every = jnp.concatenate([jnp.arange(NSETS, dtype=jnp.int32), extra])
    return jax.random.permutation(order_key, every)


def place_ends(array, own_key, least, top_value):
    longest = array.shape.index(max(array.shape))
    spots = []
    for shift in (0, 1):
        where = [jax.random.randint(jax.random.fold_in(own_key, axis), (), 0, length) for axis, length in enumerate(array.shape)]
        where[longest] = (where[longest] + shift) % array.shape[longest]
        spots.append(tuple(where))
    return array.at[spots[0]].set(least).at[spots[1]].set(top_value)


def block_levels(key, extent, cuts, smallest, largest):
    gain, own = 1.0, jax.random.fold_in(key, 6)
    for dim, blocks in cuts:
        steps = jnp.exp(jax.random.uniform(jax.random.fold_in(own, dim), (blocks,), jnp.float32, smallest / len(cuts), largest / len(cuts)))
        gain = gain * jnp.repeat(steps, extent[dim] // blocks).reshape([-1 if axis == dim else 1 for axis in range(len(extent))])
    return gain


def normal_values(key, dims, scale, most, cuts=(), kind=jnp.bfloat16):
    array = jax.random.normal(key, dims, jnp.float32) * scale
    if len(cuts) > 0:
        array = block_levels(key, dims, cuts, -0.22, 0.18) * array
    return jnp.clip(array, min=-most, max=most).astype(kind)


def setup_inputs(seed: int = 0) -> dict:
    seeds = jax.random.split(jax.random.key(seed), 7)
    return {
        "scenarios": normal_values(seeds[0], (STEPS, ROWS, FACT), 1.0, 6.0, ((1, 128),)),
        "projection": normal_values(seeds[1], (FACT, BASIS), FACT ** -0.5, 0.0390625),
        "coefs": normal_values(seeds[2], (STEPS, BASIS, NBLK, TB), (BASIS * TB * BPD // (2 * SPD)) ** -0.5, 0.0234375, ((2, 32),)),
        "exercise": jnp.clip(-0.2 + 0.2 * jax.random.uniform(seeds[3], (STEPS, NBLK, TB), jnp.float32) ** block_levels(seeds[3], (STEPS, NBLK, TB), ((1, 32),), -0.2, 0.2), -0.2, 0.0),
        "block_set": draw_block_set(jax.random.fold_in(seeds[6], 71), 0),
        "block_live": place_ends(jax.random.randint(seeds[5], (NBLK,), 1, TB + 1), jax.random.fold_in(seeds[5], 1), 1, TB).astype(jnp.int32),
    }


def reference(scenarios, projection, coefs, exercise, block_set, block_live):
    onehot = (block_set[:, None] == jnp.arange(NSETS, dtype=jnp.int32)[None, :]).astype(jnp.float32)
    live = jnp.arange(TB, dtype=jnp.int32)[None, :] < block_live[:, None]
    row_block = math.gcd(ROWS, 512)
    results = []
    for step in range(STEPS):
        basis = jnp.tanh(jnp.dot(scenarios[step], projection, preferred_element_type=jnp.float32)).astype(jnp.bfloat16)
        weights = coefs[step].reshape(BASIS, NBLK * TB)
        floor_now = exercise[step]

        def block_rows(rows):
            values = jnp.dot(rows, weights, preferred_element_type=jnp.float32).reshape(-1, NBLK, TB)
            values = jnp.where(live[None], jnp.maximum(values, floor_now[None]), 0.0)
            return jnp.dot(lax.optimization_barrier(jnp.sum(values, axis=2)), onehot, precision=lax.Precision.HIGHEST)
        netted = lax.map(block_rows, basis.reshape(ROWS // row_block, row_block, BASIS)).reshape(PATHS, REPL, NSETS)
        results.append(lax.optimization_barrier(jnp.mean(jnp.maximum(netted, 0.0), axis=0)))
    per_replicate = jnp.stack(results)
    exposure = lax.optimization_barrier(jnp.mean(per_replicate, axis=1))
    deviation = per_replicate - exposure[:, None, :]
    spread = jnp.sqrt(PATHS * lax.optimization_barrier(jnp.sum(deviation * deviation, axis=1)) / ((REPL - 1) * REPL))
    return (exposure, spread)
```

```python
import functools

import jax
import jax.numpy as jnp
from jax import lax
from jax.experimental import pallas as pl
from jax.experimental.pallas import tpu as pltpu
from jax.sharding import PartitionSpec as P

STEPS = 3
PATHS = 1024
REPL = 8
SPD = 4
SIDE = 4
BPD = 32
TB = 64
BASIS = 256
ROWS = 64
CHUNK = SIDE * ROWS
OWN = 2 * SPD
F32 = jnp.float32
BF16 = jnp.bfloat16


def ring_pairs(shift, stage):
    pairs = []
    for z in range(SIDE):
        for x in range(SIDE):
            for core in range(2):
                if (core + stage) % 2 == 0:
                    to = (z, (x + shift) % SIDE, core)
                else:
                    to = ((z + shift) % SIDE, x, core)
                pairs.append((z * 8 + x * 2 + core, to[0] * 8 + to[1] * 2 + to[2]))
    return pairs


CORE_PAIRS = [(i, i ^ 1) for i in range(2 * SIDE * SIDE)]


def shift_by(value, shift, stage):
    return lax.ppermute(value, "set", ring_pairs(shift, stage))


def swap_core(value):
    return lax.ppermute(value, "set", CORE_PAIRS)


def dot(a, b, dims):
    return lax.dot_general(a, b, (dims, ((), ())), preferred_element_type=F32)


def split(value):
    high = value.astype(BF16)
    rest = value - high.astype(F32)
    middle = rest.astype(BF16)
    low = (rest - middle.astype(F32)).astype(BF16)
    return high, middle, low


def net_kernel(rows_ref, mine_ref, other_ref, floor_ref, hot_ref, out_ref):
    for step in range(STEPS):
        rows = rows_ref[:, step].reshape(CHUNK, BASIS)
        total = None
        for half, weights in enumerate((mine_ref, other_ref)):
            sums = None
            for tile in range(BPD * TB // 256):
                cols = slice(tile * 256, (tile + 1) * 256)
                value = dot(rows, weights[step, :, cols], ((1,), (0,)))
                value = jnp.maximum(value, floor_ref[half, step, :, cols])
                both = value[:, :128] + value[:, 128:]
                sums = both if sums is None else sums + both
            for part in split(sums):
                term = dot(hot_ref[half], part, ((1,), (1,)))
                total = term if total is None else total + term
        out_ref[step] = total


def net(rows, mine, other, floors, hot):
    vmem = pl.BlockSpec(memory_space=pltpu.VMEM)
    return pl.pallas_call(
        net_kernel,
        in_specs=[vmem] * 5,
        out_specs=vmem,
        out_shape=jax.ShapeDtypeStruct((STEPS, SIDE * SIDE * OWN, CHUNK), F32),
        name="net",
    )(rows, mine, other, floors, hot)


def body(scenarios, projection, coefs, exercise, block_set, block_live):
    place = lax.axis_index("set")
    z, x, core = place // 8, (place // 2) % SIDE, place % 2

    live = jnp.arange(TB, dtype=jnp.int32)[None, :] < block_live[:, None]
    weights = jnp.where(live[None, None], coefs, 0).astype(BF16)
    weights = jnp.swapaxes(weights, 2, 3).reshape(STEPS, BASIS, TB * BPD)
    floors = jnp.swapaxes(jnp.where(live[None], exercise, 0.0), 1, 2).reshape(STEPS, 1, TB * BPD)

    basis = jnp.tanh(
        jnp.dot(
            scenarios.reshape(STEPS * ROWS, -1), projection, preferred_element_type=F32
        )
    ).astype(BF16)
    basis = basis.reshape(STEPS, ROWS, BASIS)

    first = jnp.where(core == 0, x, z)
    line = [basis] + [shift_by(basis, shift, 0) for shift in (3, 2, 1)]
    line = jnp.stack(line + line)
    line = lax.dynamic_slice_in_dim(line, SIDE - first, SIDE, 0)

    other_weights = swap_core(weights)
    other_floors = swap_core(floors)
    other_set = swap_core(block_set)

    near = (first + jnp.arange(SIDE)) % SIDE
    second = jnp.where(core == 0, z, x)
    far = (second + jnp.arange(SIDE)) % SIDE
    chip = jnp.where(
        core == 0, far[None, :] * SIDE + near[:, None], near[:, None] * SIDE + far[None, :]
    )
    ids = (chip[:, :, None] * OWN + jnp.arange(OWN)).reshape(-1)
    owners = jnp.tile(jnp.stack([block_set, other_set]), (1, SIDE))
    hot = (ids[None, :, None] == owners[:, None, :]).astype(BF16)
    both_floors = jnp.stack([floors, other_floors])

    run = functools.partial(
        net, mine=weights, other=other_weights, floors=both_floors, hot=hot
    )
    arrived = {0: line}
    for shift in (1, 3, 2):
        arrived[shift] = shift_by(line, shift, 1)
    terms = [None] * SIDE
    for shift in (0, 1, 3, 2):
        terms[shift] = run(arrived[shift]).reshape(STEPS, SIDE, SIDE, OWN, CHUNK)

    def message(near_step):
        parts = []
        for far_step in range(SIDE):
            parts.append(
                jnp.concatenate(
                    [
                        terms[(place_ - far_step) % SIDE][:, near_step, far_step]
                        for place_ in range(SIDE)
                    ],
                    axis=2,
                )
            )
        return jnp.stack(parts)

    held = message(0)
    for shift in (1, 3, 2):
        held = held + shift_by(message(shift).astype(jnp.float16), shift, 0).astype(F32)
    netted = held[0]
    for shift in (1, 3, 2):
        netted = netted + shift_by(held[shift], shift, 1)

    positive = jnp.maximum(netted, 0.0).reshape(STEPS * OWN, SIDE * CHUNK)
    pick = (jnp.arange(SIDE * CHUNK)[:, None] % REPL == jnp.arange(REPL)[None, :]).astype(F32)
    sums = jnp.dot(positive, pick, precision=lax.Precision.HIGHEST).reshape(STEPS, 2, SPD, REPL)
    kept = lax.dynamic_index_in_dim(sums, core, 1, keepdims=False)
    given = lax.dynamic_index_in_dim(sums, 1 - core, 1, keepdims=False)
    sums = kept + swap_core(given)
    total = sums
    for shift in (1, 3, 2):
        total = total + lax.ppermute(
            sums, "rep", [(i, (i + shift) % SIDE) for i in range(SIDE)]
        )
    per_replicate = total * (1.0 / PATHS)
    exposure = jnp.mean(per_replicate, axis=2)
    deviation = per_replicate - exposure[:, :, None]
    spread = jnp.sqrt(
        PATHS * jnp.sum(deviation * deviation, axis=2) / ((REPL - 1) * REPL)
    )
    return (exposure, spread)


def solution(mesh):
    return jax.shard_map(
        body,
        mesh=mesh,
        in_specs=(
            P(None, ("rep", "set"), None),
            P(),
            P(None, None, "set", None),
            P(None, "set", None),
            P("set"),
            P("set"),
        ),
        out_specs=(P(None, "set"), P(None, "set")),
        check_vma=False,
    )
```

```python
import functools

import jax
import jax.numpy as jnp
from jax import lax
from jax.experimental import pallas as pl
from jax.experimental.pallas import tpu as pltpu
from jax.sharding import PartitionSpec as P

STEPS = 3
PATHS = 1024
REPL = 8
SPD = 4
SIDE = 4
BPD = 32
TB = 64
BASIS = 256
ROWS = 64
CHUNK = SIDE * ROWS
OWN = 2 * SPD
GROUP = 4
F32 = jnp.float32
BF16 = jnp.bfloat16


def ring_pairs(shift, stage):
    pairs = []
    for z in range(SIDE):
        for x in range(SIDE):
            for core in range(2):
                if (core + stage) % 2 == 0:
                    to = (z, (x + shift) % SIDE, core)
                else:
                    to = ((z + shift) % SIDE, x, core)
                pairs.append((z * 8 + x * 2 + core, to[0] * 8 + to[1] * 2 + to[2]))
    return pairs


CORE_PAIRS = [(i, i ^ 1) for i in range(2 * SIDE * SIDE)]


def shift_by(value, shift, stage):
    return lax.ppermute(value, "set", ring_pairs(shift, stage))


def swap_core(value):
    return lax.ppermute(value, "set", CORE_PAIRS)


def dot(a, b, dims):
    return lax.dot_general(a, b, (dims, ((), ())), preferred_element_type=F32)


def net_kernel(
    live_ref, rows_ref, mine_ref, other_ref, floor_ref, hot_ref, out_ref, sums_ref, held_ref, sems
):
    copies = [
        [
            pltpu.make_async_copy(source.at[step], held_ref.at[step, half], sems.at[step, half])
            for half, source in enumerate((mine_ref, other_ref))
        ]
        for step in range(STEPS)
    ]
    for pair in copies:
        for copy in pair:
            copy.start()
    trade = lax.broadcasted_iota(jnp.int32, (TB, CHUNK), 0)
    for step in range(STEPS):
        rows = rows_ref[:, step].reshape(CHUNK, BASIS)
        for half in range(2):
            copies[step][half].wait()
            for first in range(0, BPD, GROUP):
                trades = slice(first * TB, (first + GROUP) * TB)
                values = dot(held_ref[step, half, trades, :], rows, ((1,), (1,)))
                for block in range(GROUP):
                    spot = half * BPD + first + block
                    floor = floor_ref[step, :, spot : spot + 1]
                    value = jnp.maximum(values[block * TB : (block + 1) * TB], floor)
                    value = jnp.where(trade < live_ref[spot], value, 0.0)
                    sums = value[:8]
                    for part in range(8, TB, 8):
                        sums = sums + value[part : part + 8]
                    sums_ref[spot * 8 : spot * 8 + 8, :] = sums
        sums = sums_ref[...]
        high = sums.astype(BF16)
        low = (sums - high.astype(F32)).astype(BF16)
        hot = hot_ref[...]
        out_ref[step] = dot(hot, high, ((1,), (0,))) + dot(hot, low, ((1,), (0,)))


VMEM = pl.BlockSpec(memory_space=pltpu.VMEM)
SMEM = pl.BlockSpec(memory_space=pltpu.SMEM)
ANY = pl.BlockSpec(memory_space=pl.ANY)


def net(rows, live, mine, other, floors, hot):
    mine = pltpu.with_memory_space_constraint(mine, pltpu.HBM)
    return pl.pallas_call(
        net_kernel,
        in_specs=[SMEM, VMEM, ANY, ANY, VMEM, VMEM],
        out_specs=VMEM,
        out_shape=jax.ShapeDtypeStruct((STEPS, SIDE * SIDE * OWN, CHUNK), F32),
        scratch_shapes=[
            pltpu.VMEM((2 * BPD * 8, CHUNK), F32),
            pltpu.VMEM((STEPS, 2, BPD * TB, BASIS), BF16),
            pltpu.SemaphoreType.DMA((STEPS, 2)),
        ],
        compiler_params=pltpu.CompilerParams(vmem_limit_bytes=20 << 20),
        cost_estimate=pl.CostEstimate(
            flops=4 * STEPS * CHUNK * BPD * TB * BASIS, bytes_accessed=1 << 20, transcendentals=0
        ),
        name="net",
    )(live, rows, mine, other, floors, hot)


def line_kernel(first_ref, *refs):
    out_ref = refs[-1]
    for step in range(SIDE):
        out_ref[lax.rem(first_ref[0] + step, SIDE)] = refs[step][...]


def make_line(first, parts):
    return pl.pallas_call(
        line_kernel,
        in_specs=[SMEM] + [pl.BlockSpec()] * SIDE,
        out_specs=pl.BlockSpec(),
        out_shape=jax.ShapeDtypeStruct((SIDE, STEPS, ROWS, BASIS), BF16),
        compiler_params=pltpu.CompilerParams(vmem_limit_bytes=4 << 20),
        name="line",
    )(first.reshape(1), *parts)


def body(scenarios, projection, coefs, exercise, block_set, block_live):
    place = lax.axis_index("set")
    z, x, core = place // 8, (place // 2) % SIDE, place % 2

    basis = jnp.tanh(
        jnp.dot(
            scenarios.reshape(STEPS * ROWS, -1), projection, preferred_element_type=F32
        )
    ).astype(BF16)
    basis = basis.reshape(STEPS, ROWS, BASIS)
    weights = jnp.transpose(coefs, (0, 2, 3, 1)).reshape(STEPS, BPD * TB, BASIS)

    first = jnp.where(core == 0, x, z)
    line = make_line(first, [basis] + [shift_by(basis, shift, 0) for shift in (3, 2, 1)])

    other_weights = swap_core(weights)
    other_floors = swap_core(exercise)
    blocks = jnp.stack([block_set, block_live])
    blocks = jnp.concatenate([blocks, swap_core(blocks)], axis=1)

    near = (first + jnp.arange(SIDE)) % SIDE
    second = jnp.where(core == 0, z, x)
    far = (second + jnp.arange(SIDE)) % SIDE
    chip = jnp.where(
        core == 0, far[None, :] * SIDE + near[:, None], near[:, None] * SIDE + far[None, :]
    )
    ids = (chip[:, :, None] * OWN + jnp.arange(OWN)).reshape(-1)
    owners = jnp.repeat(blocks[0], 8)
    hot = (ids[:, None] == owners[None, :]).astype(BF16)
    both_floors = jnp.swapaxes(jnp.concatenate([exercise, other_floors], axis=1), 1, 2)

    run = functools.partial(
        net, live=blocks[1], mine=weights, other=other_weights, floors=both_floors, hot=hot
    )
    arrived = {shift: shift_by(line, shift, 1) for shift in (1, 3, 2)}
    terms, sent = {}, {}
    rows = line
    for shift, following in ((0, 1), (1, 3), (3, 2), (2, None)):
        terms[shift] = run(rows).reshape(STEPS, SIDE, SIDE, OWN, CHUNK)
        sent[shift] = terms[shift][:, 1:].astype(jnp.float16)
        if following:
            rows, sent[shift] = lax.optimization_barrier((arrived[following], sent[shift]))

    def message(values, near_step):
        return jnp.stack(
            [
                jnp.concatenate(
                    [values[(spot - far_step) % SIDE][:, near_step, far_step] for spot in range(SIDE)],
                    axis=2,
                )
                for far_step in range(SIDE)
            ]
        )

    held = message(terms, 0)
    for shift in (1, 3, 2):
        held = held + shift_by(message(sent, shift - 1), shift, 0).astype(F32)
    netted = held[0]
    for shift in (1, 3, 2):
        half = (held[shift] * 0.5).astype(jnp.float16)
        netted = netted + shift_by(half, shift, 1).astype(F32) * 2.0

    positive = jnp.maximum(netted, 0.0).reshape(STEPS * OWN, SIDE * CHUNK)
    pick = (jnp.arange(SIDE * CHUNK)[:, None] % REPL == jnp.arange(REPL)[None, :]).astype(F32)
    sums = jnp.dot(positive, pick, precision=lax.Precision.HIGHEST).reshape(STEPS, 2, SPD, REPL)
    kept = lax.dynamic_index_in_dim(sums, core, 1, keepdims=False)
    given = lax.dynamic_index_in_dim(sums, 1 - core, 1, keepdims=False)
    sums = kept + swap_core(given)
    total = sums
    for shift in (1, 3, 2):
        total = total + lax.ppermute(
            sums, "rep", [(i, (i + shift) % SIDE) for i in range(SIDE)]
        )
    per_replicate = total * (1.0 / PATHS)
    exposure = jnp.mean(per_replicate, axis=2)
    deviation = per_replicate - exposure[:, :, None]
    spread = jnp.sqrt(
        PATHS * jnp.sum(deviation * deviation, axis=2) / ((REPL - 1) * REPL)
    )
    return (exposure, spread)


def solution(mesh):
    return jax.shard_map(
        body,
        mesh=mesh,
        in_specs=(
            P(None, ("rep", "set"), None),
            P(),
            P(None, None, "set", None),
            P(None, "set", None),
            P("set"),
            P("set"),
        ),
        out_specs=(P(None, "set"), P(None, "set")),
        check_vma=False,
    )
```

```python
import jax
import jax.numpy as jnp
from jax import lax
from jax.experimental import pallas as pl
from jax.experimental.pallas import tpu as pltpu
from jax.sharding import PartitionSpec as P

STEPS = 3
PATHS = 1024
REPL = 8
SPD = 4
SIDE = 4
BPD = 32
TB = 64
BASIS = 256
ROWS = 64
CHUNK = SIDE * ROWS
OWN = 2 * SPD
GROUP = 4
F32 = jnp.float32
BF16 = jnp.bfloat16


def ring_pairs(shift, stage):
    pairs = []
    for z in range(SIDE):
        for x in range(SIDE):
            for core in range(2):
                if (core + stage) % 2 == 0:
                    to = (z, (x + shift) % SIDE, core)
                else:
                    to = ((z + shift) % SIDE, x, core)
                pairs.append((z * 8 + x * 2 + core, to[0] * 8 + to[1] * 2 + to[2]))
    return pairs


CORE_PAIRS = [(i, i ^ 1) for i in range(2 * SIDE * SIDE)]


def shift_by(value, shift, stage):
    return lax.ppermute(value, "set", ring_pairs(shift, stage))


def swap_core(value):
    return lax.ppermute(value, "set", CORE_PAIRS)


def dot(a, b, dims):
    return lax.dot_general(a, b, (dims, ((), ())), preferred_element_type=F32)


def net_rows(live_ref, rows_ref, floor_ref, hot_ref, held_ref, out_ref, sums_ref, copies=None):
    trade = lax.broadcasted_iota(jnp.int32, (TB, CHUNK), 0)
    for step in range(STEPS):
        rows = rows_ref[:, step].reshape(CHUNK, BASIS)
        for half in range(2):
            if copies:
                copies[step][half].wait()
            for first in range(0, BPD, GROUP):
                trades = slice(first * TB, (first + GROUP) * TB)
                values = dot(held_ref[step, half, trades, :], rows, ((1,), (1,)))
                for block in range(GROUP):
                    spot = half * BPD + first + block
                    floor = floor_ref[step, :, spot : spot + 1]
                    value = jnp.maximum(values[block * TB : (block + 1) * TB], floor)
                    value = jnp.where(trade < live_ref[spot], value, 0.0)
                    sums = value[:8]
                    for part in range(8, TB, 8):
                        sums = sums + value[part : part + 8]
                    sums_ref[spot * 8 : spot * 8 + 8, :] = sums
        sums = sums_ref[...]
        high = sums.astype(BF16)
        low = (sums - high.astype(F32)).astype(BF16)
        hot = hot_ref[...]
        out_ref[step] = dot(hot, high, ((1,), (0,))) + dot(hot, low, ((1,), (0,)))


def net_first_kernel(
    live_ref, rows_ref, mine_ref, other_ref, floor_ref, hot_ref, out_ref, held_ref, sums_ref, sems
):
    copies = [
        [
            pltpu.make_async_copy(source.at[step], held_ref.at[step, half], sems.at[step, half])
            for half, source in enumerate((mine_ref, other_ref))
        ]
        for step in range(STEPS)
    ]
    for pair in copies:
        for copy in pair:
            copy.start()
    net_rows(live_ref, rows_ref, floor_ref, hot_ref, held_ref, out_ref, sums_ref, copies)


def net_next_kernel(live_ref, rows_ref, held_ref, floor_ref, hot_ref, out_ref, sums_ref):
    net_rows(live_ref, rows_ref, floor_ref, hot_ref, held_ref, out_ref, sums_ref)


VMEM = pl.BlockSpec(memory_space=pltpu.VMEM)
SMEM = pl.BlockSpec(memory_space=pltpu.SMEM)
ANY = pl.BlockSpec(memory_space=pl.ANY)


TERMS = (STEPS, SIDE * SIDE * OWN, CHUNK)
HELD = (STEPS, 2, BPD * TB, BASIS)


def net_first(rows, live, mine, other, floors, hot):
    mine = pltpu.with_memory_space_constraint(mine, pltpu.HBM)
    return pl.pallas_call(
        net_first_kernel,
        in_specs=[SMEM, VMEM, ANY, ANY, VMEM, VMEM],
        out_specs=(VMEM, VMEM),
        out_shape=(jax.ShapeDtypeStruct(TERMS, F32), pltpu.VMEM(HELD, BF16)),
        scratch_shapes=[
            pltpu.VMEM((2 * BPD * 8, CHUNK), F32),
            pltpu.SemaphoreType.DMA((STEPS, 2)),
        ],
        compiler_params=pltpu.CompilerParams(vmem_limit_bytes=20 << 20),
        name="net_first",
    )(live, rows, mine, other, floors, hot)


def net_next(rows, live, held, floors, hot):
    held = pltpu.with_memory_space_constraint(held, pltpu.VMEM)
    return pl.pallas_call(
        net_next_kernel,
        in_specs=[SMEM, VMEM, VMEM, VMEM, VMEM],
        out_specs=VMEM,
        out_shape=jax.ShapeDtypeStruct(TERMS, F32),
        scratch_shapes=[pltpu.VMEM((2 * BPD * 8, CHUNK), F32)],
        compiler_params=pltpu.CompilerParams(vmem_limit_bytes=12 << 20),
        name="net_next",
    )(live, rows, held, floors, hot)


def line_kernel(first_ref, *refs):
    out_ref = refs[-1]
    for step in range(SIDE):
        out_ref[lax.rem(first_ref[0] + step, SIDE)] = refs[step][...]


def make_line(first, parts):
    return pl.pallas_call(
        line_kernel,
        in_specs=[SMEM] + [pl.BlockSpec()] * SIDE,
        out_specs=pl.BlockSpec(),
        out_shape=jax.ShapeDtypeStruct((SIDE, STEPS, ROWS, BASIS), BF16),
        compiler_params=pltpu.CompilerParams(vmem_limit_bytes=4 << 20),
        name="line",
    )(first.reshape(1), *parts)


def body(scenarios, projection, coefs, exercise, block_set, block_live):
    place = lax.axis_index("set")
    z, x, core = place // 8, (place // 2) % SIDE, place % 2

    basis = jnp.tanh(
        jnp.dot(
            scenarios.reshape(STEPS * ROWS, -1), projection, preferred_element_type=F32
        )
    ).astype(BF16)
    basis = basis.reshape(STEPS, ROWS, BASIS)
    weights = jnp.transpose(coefs, (0, 2, 3, 1)).reshape(STEPS, BPD * TB, BASIS)

    first = jnp.where(core == 0, x, z)
    line = make_line(first, [basis] + [shift_by(basis, shift, 0) for shift in (3, 2, 1)])

    other_weights = swap_core(weights)
    other_floors = swap_core(exercise)
    blocks = jnp.stack([block_set, block_live])
    blocks = jnp.concatenate([blocks, swap_core(blocks)], axis=1)

    near = (first + jnp.arange(SIDE)) % SIDE
    second = jnp.where(core == 0, z, x)
    far = (second + jnp.arange(SIDE)) % SIDE
    chip = jnp.where(
        core == 0, far[None, :] * SIDE + near[:, None], near[:, None] * SIDE + far[None, :]
    )
    ids = (chip[:, :, None] * OWN + jnp.arange(OWN)).reshape(-1)
    owners = jnp.repeat(blocks[0], 8)
    hot = (ids[:, None] == owners[None, :]).astype(BF16)
    both_floors = jnp.swapaxes(jnp.concatenate([exercise, other_floors], axis=1), 1, 2)

    arrived = {shift: shift_by(line, shift, 1) for shift in (1, 3, 2)}
    terms, sent = {}, {}
    rows = line
    for shift, following in ((0, 1), (1, 3), (3, 2), (2, None)):
        if shift == 0:
            term, held = net_first(rows, blocks[1], weights, other_weights, both_floors, hot)
        else:
            term = net_next(rows, blocks[1], held, both_floors, hot)
        terms[shift] = term.reshape(STEPS, SIDE, SIDE, OWN, CHUNK)
        sent[shift] = terms[shift][:, 1:].astype(jnp.float16)
        if following:
            rows, sent[shift] = lax.optimization_barrier((arrived[following], sent[shift]))

    def message(values, near_step):
        return jnp.stack(
            [
                jnp.concatenate(
                    [values[(spot - far_step) % SIDE][:, near_step, far_step] for spot in range(SIDE)],
                    axis=2,
                )
                for far_step in range(SIDE)
            ]
        )

    held = message(terms, 0)
    for shift in (1, 3, 2):
        held = held + shift_by(message(sent, shift - 1), shift, 0).astype(F32)
    netted = held[0]
    for shift in (1, 3, 2):
        half = (held[shift] * 0.5).astype(jnp.float16)
        netted = netted + shift_by(half, shift, 1).astype(F32) * 2.0

    positive = jnp.maximum(netted, 0.0).reshape(STEPS * OWN, SIDE * CHUNK)
    pick = (jnp.arange(SIDE * CHUNK)[:, None] % REPL == jnp.arange(REPL)[None, :]).astype(F32)
    sums = jnp.dot(positive, pick, precision=lax.Precision.HIGHEST).reshape(STEPS, 2, SPD, REPL)
    kept = lax.dynamic_index_in_dim(sums, core, 1, keepdims=False)
    given = lax.dynamic_index_in_dim(sums, 1 - core, 1, keepdims=False)
    sums = kept + swap_core(given)
    total = sums
    for shift in (1, 3, 2):
        total = total + lax.ppermute(
            sums, "rep", [(i, (i + shift) % SIDE) for i in range(SIDE)]
        )
    per_replicate = total * (1.0 / PATHS)
    exposure = jnp.mean(per_replicate, axis=2)
    deviation = per_replicate - exposure[:, :, None]
    spread = jnp.sqrt(
        PATHS * jnp.sum(deviation * deviation, axis=2) / ((REPL - 1) * REPL)
    )
    return (exposure, spread)


def solution(mesh):
    return jax.shard_map(
        body,
        mesh=mesh,
        in_specs=(
            P(None, ("rep", "set"), None),
            P(),
            P(None, None, "set", None),
            P(None, "set", None),
            P("set"),
            P("set"),
        ),
        out_specs=(P(None, "set"), P(None, "set")),
        check_vma=False,
    )
```

```python
import jax
import jax.numpy as jnp
from jax import lax
from jax.experimental import pallas as pl
from jax.experimental.pallas import tpu as pltpu
from jax.sharding import PartitionSpec as P

STEPS = 3
PATHS = 1024
REPL = 8
SPD = 4
SIDE = 4
BPD = 32
TB = 64
BASIS = 256
ROWS = 64
CHUNK = SIDE * ROWS
OWN = 2 * SPD
GROUP = 4
F32 = jnp.float32
BF16 = jnp.bfloat16


def ring_pairs(shift, stage):
    pairs = []
    for z in range(SIDE):
        for x in range(SIDE):
            for core in range(2):
                if (core + stage) % 2 == 0:
                    to = (z, (x + shift) % SIDE, core)
                else:
                    to = ((z + shift) % SIDE, x, core)
                pairs.append((z * 8 + x * 2 + core, to[0] * 8 + to[1] * 2 + to[2]))
    return pairs


CORE_PAIRS = [(i, i ^ 1) for i in range(2 * SIDE * SIDE)]


def shift_by(value, shift, stage):
    return lax.ppermute(value, "set", ring_pairs(shift, stage))


def swap_core(value):
    return lax.ppermute(value, "set", CORE_PAIRS)


def dot(a, b, dims):
    return lax.dot_general(a, b, (dims, ((), ())), preferred_element_type=F32)


def net_rows(
    live_ref, rows_ref, floor_refs, hot_ref, held_ref, out_ref, sums_ref, copies=None
):
    trade = lax.broadcasted_iota(jnp.int32, (TB, CHUNK), 0)
    for step in range(STEPS):
        rows = rows_ref[:, step].reshape(CHUNK, BASIS)
        if copies and step + 1 < STEPS:
            for copy in copies[step + 1]:
                copy.start()
        for half in range(2):
            floors = jnp.transpose(floor_refs[half][step])
            if copies:
                copies[step][half].wait()
            for first in range(0, BPD, GROUP):
                trades = slice(first * TB, (first + GROUP) * TB)
                values = dot(held_ref[step, half, trades, :], rows, ((1,), (1,)))
                for block in range(GROUP):
                    spot = half * BPD + first + block
                    floor = floors[:, first + block : first + block + 1]
                    value = jnp.maximum(values[block * TB : (block + 1) * TB], floor)
                    value = jnp.where(trade < live_ref[spot], value, 0.0)
                    sums = value[:8]
                    for part in range(8, TB, 8):
                        sums = sums + value[part : part + 8]
                    sums_ref[spot * 8 : spot * 8 + 8, :] = sums
        sums = sums_ref[...]
        high = sums.astype(BF16)
        low = (sums - high.astype(F32)).astype(BF16)
        hot = hot_ref[...]
        out_ref[step] = dot(hot, high, ((1,), (0,))) + dot(hot, low, ((1,), (0,)))


def net_first_kernel(
    live_ref,
    rows_ref,
    mine_ref,
    other_ref,
    my_floor_ref,
    other_floor_ref,
    hot_ref,
    out_ref,
    held_ref,
    sums_ref,
    sems,
):
    copies = [
        [
            pltpu.make_async_copy(source.at[step], held_ref.at[step, half], sems.at[step, half])
            for half, source in enumerate((mine_ref, other_ref))
        ]
        for step in range(STEPS)
    ]
    for copy in copies[0]:
        copy.start()
    floors = (my_floor_ref, other_floor_ref)
    net_rows(live_ref, rows_ref, floors, hot_ref, held_ref, out_ref, sums_ref, copies)


def net_next_kernel(
    live_ref, rows_ref, held_ref, my_floor_ref, other_floor_ref, hot_ref, out_ref, sums_ref
):
    floors = (my_floor_ref, other_floor_ref)
    net_rows(live_ref, rows_ref, floors, hot_ref, held_ref, out_ref, sums_ref)


VMEM = pl.BlockSpec(memory_space=pltpu.VMEM)
SMEM = pl.BlockSpec(memory_space=pltpu.SMEM)
ANY = pl.BlockSpec(memory_space=pl.ANY)


TERMS = (STEPS, SIDE * SIDE * OWN, CHUNK)
HELD = (STEPS, 2, BPD * TB, BASIS)


def net_first(rows, live, mine, other, floors, hot):
    mine = pltpu.with_memory_space_constraint(mine, pltpu.HBM)
    return pl.pallas_call(
        net_first_kernel,
        in_specs=[SMEM, VMEM, ANY, ANY, VMEM, VMEM, VMEM],
        out_specs=(VMEM, VMEM),
        out_shape=(jax.ShapeDtypeStruct(TERMS, F32), pltpu.VMEM(HELD, BF16)),
        scratch_shapes=[
            pltpu.VMEM((2 * BPD * 8, CHUNK), F32),
            pltpu.SemaphoreType.DMA((STEPS, 2)),
        ],
        compiler_params=pltpu.CompilerParams(vmem_limit_bytes=20 << 20),
        name="net_first",
    )(live, rows, mine, other, *floors, hot)


def net_next(rows, live, held, floors, hot):
    held = pltpu.with_memory_space_constraint(held, pltpu.VMEM)
    return pl.pallas_call(
        net_next_kernel,
        in_specs=[SMEM] + [VMEM] * 5,
        out_specs=VMEM,
        out_shape=jax.ShapeDtypeStruct(TERMS, F32),
        scratch_shapes=[pltpu.VMEM((2 * BPD * 8, CHUNK), F32)],
        compiler_params=pltpu.CompilerParams(vmem_limit_bytes=12 << 20),
        name="net_next",
    )(live, rows, held, *floors, hot)


def line_kernel(first_ref, *refs):
    out_ref = refs[-1]
    for step in range(SIDE):
        out_ref[lax.rem(first_ref[0] + step, SIDE)] = refs[step][...]


def make_line(first, parts):
    return pl.pallas_call(
        line_kernel,
        in_specs=[SMEM] + [pl.BlockSpec()] * SIDE,
        out_specs=pl.BlockSpec(),
        out_shape=jax.ShapeDtypeStruct((SIDE, STEPS, ROWS, BASIS), BF16),
        compiler_params=pltpu.CompilerParams(vmem_limit_bytes=4 << 20),
        name="line",
    )(first.reshape(1), *parts)


def body(scenarios, projection, coefs, exercise, block_set, block_live):
    place = lax.axis_index("set")
    z, x, core = place // 8, (place // 2) % SIDE, place % 2

    basis = jnp.tanh(
        jnp.dot(
            scenarios.reshape(STEPS * ROWS, -1), projection, preferred_element_type=F32
        )
    ).astype(BF16)
    basis = basis.reshape(STEPS, ROWS, BASIS)
    weights = jnp.transpose(coefs, (0, 2, 3, 1)).reshape(STEPS, BPD * TB, BASIS)

    first = jnp.where(core == 0, x, z)
    line = make_line(first, [basis] + [shift_by(basis, shift, 0) for shift in (3, 2, 1)])

    other_weights = swap_core(weights)
    other_floors = swap_core(exercise)
    blocks = jnp.stack([block_set, block_live])
    blocks = jnp.concatenate([blocks, swap_core(blocks)], axis=1)

    near = (first + jnp.arange(SIDE)) % SIDE
    second = jnp.where(core == 0, z, x)
    far = (second + jnp.arange(SIDE)) % SIDE
    chip = jnp.where(
        core == 0, far[None, :] * SIDE + near[:, None], near[:, None] * SIDE + far[None, :]
    )
    ids = (chip[:, :, None] * OWN + jnp.arange(OWN)).reshape(-1)
    owners = jnp.repeat(blocks[0], 8)
    hot = (ids[:, None] == owners[None, :]).astype(BF16)
    both_floors = (exercise, other_floors)

    arrived = {shift: shift_by(line, shift, 1) for shift in (1, 3, 2)}
    terms, sent = {}, {}
    rows = line
    for shift, following in ((0, 1), (1, 3), (3, 2), (2, None)):
        if shift == 0:
            term, held = net_first(rows, blocks[1], weights, other_weights, both_floors, hot)
        else:
            term = net_next(rows, blocks[1], held, both_floors, hot)
        terms[shift] = term.reshape(STEPS, SIDE, SIDE, OWN, CHUNK)
        sent[shift] = terms[shift][:, 1:].astype(jnp.float16)
        if following:
            rows, sent[shift] = lax.optimization_barrier((arrived[following], sent[shift]))

    def message(values, near_step):
        return jnp.stack(
            [
                jnp.concatenate(
                    [values[(spot - far_step) % SIDE][:, near_step, far_step] for spot in range(SIDE)],
                    axis=2,
                )
                for far_step in range(SIDE)
            ]
        )

    held = message(terms, 0)
    for shift in (1, 3, 2):
        held = held + shift_by(message(sent, shift - 1), shift, 0).astype(F32)
    netted = held[0]
    for shift in (1, 3, 2):
        half = (held[shift] * 0.5).astype(jnp.float16)
        netted = netted + shift_by(half, shift, 1).astype(F32) * 2.0

    positive = jnp.maximum(netted, 0.0).reshape(STEPS * OWN, SIDE * CHUNK)
    pick = (jnp.arange(SIDE * CHUNK)[:, None] % REPL == jnp.arange(REPL)[None, :]).astype(F32)
    sums = jnp.dot(positive, pick, precision=lax.Precision.HIGHEST).reshape(STEPS, 2, SPD, REPL)
    kept = lax.dynamic_index_in_dim(sums, core, 1, keepdims=False)
    given = lax.dynamic_index_in_dim(sums, 1 - core, 1, keepdims=False)
    sums = kept + swap_core(given)
    total = sums
    for shift in (1, 3, 2):
        total = total + lax.ppermute(
            sums, "rep", [(i, (i + shift) % SIDE) for i in range(SIDE)]
        )
    per_replicate = total * (1.0 / PATHS)
    exposure = jnp.mean(per_replicate, axis=2)
    deviation = per_replicate - exposure[:, :, None]
    spread = jnp.sqrt(
        PATHS * jnp.sum(deviation * deviation, axis=2) / ((REPL - 1) * REPL)
    )
    return (exposure, spread)


def solution(mesh):
    return jax.shard_map(
        body,
        mesh=mesh,
        in_specs=(
            P(None, ("rep", "set"), None),
            P(),
            P(None, None, "set", None),
            P(None, "set", None),
            P("set"),
            P("set"),
        ),
        out_specs=(P(None, "set"), P(None, "set")),
        check_vma=False,
    )
```

```python
import jax
import jax.numpy as jnp
from jax import lax
from jax.experimental import pallas as pl
from jax.experimental.pallas import tpu as pltpu
from jax.sharding import PartitionSpec as P

STEPS = 3
PATHS = 1024
REPL = 8
SPD = 4
SIDE = 4
BPD = 32
TB = 64
BASIS = 256
FACTORS = 20000
FACTOR_TILE = 6784
ROWS = 64
CHUNK = SIDE * ROWS
OWN = 2 * SPD
GROUP = 4
F32 = jnp.float32
BF16 = jnp.bfloat16


def ring_pairs(shift, stage):
    pairs = []
    for z in range(SIDE):
        for x in range(SIDE):
            for core in range(2):
                if (core + stage) % 2 == 0:
                    to = (z, (x + shift) % SIDE, core)
                else:
                    to = ((z + shift) % SIDE, x, core)
                pairs.append((z * 8 + x * 2 + core, to[0] * 8 + to[1] * 2 + to[2]))
    return pairs


CORE_PAIRS = [(i, i ^ 1) for i in range(2 * SIDE * SIDE)]


def shift_by(value, shift, stage):
    return lax.ppermute(value, "set", ring_pairs(shift, stage))


def swap_core(value):
    return lax.ppermute(value, "set", CORE_PAIRS)


def dot(a, b, dims):
    return lax.dot_general(a, b, (dims, ((), ())), preferred_element_type=F32)


def net_rows(
    live_ref, rows_ref, held_ref, other_ref, my_floor_ref, other_floor_ref, hot_ref, out_ref, sums_ref,
    copies=None,
):
    trade = lax.broadcasted_iota(jnp.int32, (TB, CHUNK), 0)
    for step in range(STEPS):
        rows = rows_ref[:, step].reshape(CHUNK, BASIS)
        for half, (weights, floors) in enumerate(
            ((held_ref, my_floor_ref), (other_ref, other_floor_ref))
        ):
            if copies and half == 0:
                copies[step].wait()
            floors = jnp.transpose(floors[step])
            for first in range(0, BPD, GROUP):
                trades = slice(first * TB, (first + GROUP) * TB)
                values = dot(weights[step, trades, :], rows, ((1,), (1,)))
                for block in range(GROUP):
                    spot = half * BPD + first + block
                    floor = floors[:, first + block : first + block + 1]
                    value = jnp.maximum(values[block * TB : (block + 1) * TB], floor)
                    value = jnp.where(trade < live_ref[spot], value, 0.0)
                    sums = value[:8]
                    for part in range(8, TB, 8):
                        sums = sums + value[part : part + 8]
                    sums_ref[spot * 8 : spot * 8 + 8, :] = sums
        sums = sums_ref[...]
        high = sums.astype(BF16)
        low = (sums - high.astype(F32)).astype(BF16)
        hot = hot_ref[...]
        out_ref[step] = dot(hot, high, ((1,), (0,))) + dot(hot, low, ((1,), (0,)))


def net_first_kernel(
    live_ref, rows_ref, mine_ref, other_ref, my_floor_ref, other_floor_ref, hot_ref, out_ref, held_ref,
    sums_ref, sems,
):
    copies = [
        pltpu.make_async_copy(mine_ref.at[step], held_ref.at[step], sems.at[step])
        for step in range(STEPS)
    ]
    for copy in copies:
        copy.start()
    net_rows(
        live_ref, rows_ref, held_ref, other_ref, my_floor_ref, other_floor_ref, hot_ref, out_ref,
        sums_ref, copies,
    )


def net_next_kernel(*refs):
    net_rows(*refs)


VMEM = pl.BlockSpec(memory_space=pltpu.VMEM)
SMEM = pl.BlockSpec(memory_space=pltpu.SMEM)
HBM = pl.BlockSpec(memory_space=pltpu.HBM)


TERMS = (STEPS, SIDE * SIDE * OWN, CHUNK)
HELD = (STEPS, BPD * TB, BASIS)


def net_first(rows, live, mine, other, my_floors, other_floors, hot):
    mine = pltpu.with_memory_space_constraint(mine, pltpu.HBM)
    other = pltpu.with_memory_space_constraint(other, pltpu.VMEM)
    return pl.pallas_call(
        net_first_kernel,
        in_specs=[SMEM, VMEM, HBM, VMEM, VMEM, VMEM, VMEM],
        out_specs=(VMEM, VMEM),
        out_shape=(jax.ShapeDtypeStruct(TERMS, F32), pltpu.VMEM(HELD, BF16)),
        scratch_shapes=[
            pltpu.VMEM((2 * BPD * 8, CHUNK), F32),
            pltpu.SemaphoreType.DMA((STEPS,)),
        ],
        compiler_params=pltpu.CompilerParams(vmem_limit_bytes=12 << 20),
        name="net_first",
    )(live, rows, mine, other, my_floors, other_floors, hot)


def net_next(rows, live, held, other, my_floors, other_floors, hot):
    held = pltpu.with_memory_space_constraint(held, pltpu.VMEM)
    other = pltpu.with_memory_space_constraint(other, pltpu.VMEM)
    return pl.pallas_call(
        net_next_kernel,
        in_specs=[SMEM] + [VMEM] * 6,
        out_specs=VMEM,
        out_shape=jax.ShapeDtypeStruct(TERMS, F32),
        scratch_shapes=[pltpu.VMEM((2 * BPD * 8, CHUNK), F32)],
        compiler_params=pltpu.CompilerParams(vmem_limit_bytes=12 << 20),
        name="net_next",
    )(live, rows, held, other, my_floors, other_floors, hot)


def basis_kernel(scenarios_ref, projection_ref, out_ref, sums_ref):
    step = pl.program_id(0)
    last = pl.num_programs(0) - 1
    width = FACTORS - (-(-FACTORS // FACTOR_TILE) - 1) * FACTOR_TILE
    rows = STEPS * ROWS

    @pl.when(step == 0)
    def _():
        sums_ref[...] = jnp.zeros_like(sums_ref)

    @pl.when(step < last)
    def _():
        tile = scenarios_ref[...].reshape(rows, FACTOR_TILE)
        sums_ref[...] += dot(tile, projection_ref[...], ((1,), (0,)))

    @pl.when(step == last)
    def _():
        tile = scenarios_ref[:, :, :width].reshape(rows, width)
        sums = sums_ref[...] + dot(tile, projection_ref[:width, :], ((1,), (0,)))
        out_ref[...] = jnp.tanh(sums).astype(BF16).reshape(STEPS, ROWS, BASIS)


def make_basis(scenarios, projection):
    scenarios = pltpu.with_memory_space_constraint(scenarios, pltpu.HBM)
    projection = pltpu.with_memory_space_constraint(projection, pltpu.HBM)
    return pl.pallas_call(
        basis_kernel,
        grid=(-(-FACTORS // FACTOR_TILE),),
        in_specs=[
            pl.BlockSpec((STEPS, ROWS, FACTOR_TILE), lambda k: (0, 0, k)),
            pl.BlockSpec((FACTOR_TILE, BASIS), lambda k: (k, 0)),
        ],
        out_specs=pl.BlockSpec((STEPS, ROWS, BASIS), lambda k: (0, 0, 0)),
        out_shape=jax.ShapeDtypeStruct((STEPS, ROWS, BASIS), BF16),
        scratch_shapes=[pltpu.VMEM((STEPS * ROWS, BASIS), F32)],
        compiler_params=pltpu.CompilerParams(vmem_limit_bytes=24 << 20),
        name="basis",
    )(scenarios, projection)


def line_kernel(first_ref, *refs):
    out_ref = refs[-1]
    for step in range(SIDE):
        out_ref[lax.rem(first_ref[0] + step, SIDE)] = refs[step][...]


def make_line(first, parts):
    return pl.pallas_call(
        line_kernel,
        in_specs=[SMEM] + [pl.BlockSpec()] * SIDE,
        out_specs=pl.BlockSpec(),
        out_shape=jax.ShapeDtypeStruct((SIDE, STEPS, ROWS, BASIS), BF16),
        compiler_params=pltpu.CompilerParams(vmem_limit_bytes=4 << 20),
        name="line",
    )(first.reshape(1), *parts)


def body(scenarios, projection, coefs, exercise, block_set, block_live):
    place = lax.axis_index("set")
    z, x, core = place // 8, (place // 2) % SIDE, place % 2

    basis = make_basis(scenarios, projection)
    weights = jnp.transpose(coefs, (0, 2, 3, 1)).reshape(STEPS, BPD * TB, BASIS)

    first = jnp.where(core == 0, x, z)
    line = make_line(first, [basis] + [shift_by(basis, shift, 0) for shift in (3, 2, 1)])

    other_weights = swap_core(weights)
    other_floors = swap_core(exercise)
    blocks = jnp.stack([block_set, block_live])
    blocks = jnp.concatenate([blocks, swap_core(blocks)], axis=1)

    near = (first + jnp.arange(SIDE)) % SIDE
    second = jnp.where(core == 0, z, x)
    far = (second + jnp.arange(SIDE)) % SIDE
    chip = jnp.where(
        core == 0, far[None, :] * SIDE + near[:, None], near[:, None] * SIDE + far[None, :]
    )
    ids = (chip[:, :, None] * OWN + jnp.arange(OWN)).reshape(-1)
    owners = jnp.repeat(blocks[0], 8)
    hot = (ids[:, None] == owners[None, :]).astype(BF16)

    arrived = {shift: shift_by(line, shift, 1) for shift in (1, 3, 2)}
    terms, sent = {}, {}
    rows = line
    for shift, following in ((0, 3), (3, 2), (2, 1), (1, None)):
        fixed = (other_weights, exercise, other_floors, hot)
        if shift == 0:
            term, held = net_first(rows, blocks[1], weights, *fixed)
        else:
            term = net_next(rows, blocks[1], held, *fixed)
        terms[shift] = term.reshape(STEPS, SIDE, SIDE, OWN, CHUNK)
        sent[shift] = terms[shift][:, 1:].astype(jnp.float16)
        if following:
            rows, sent[shift] = lax.optimization_barrier((arrived[following], sent[shift]))

    def message(values, near_step):
        return jnp.stack(
            [
                jnp.concatenate(
                    [values[(spot - far_step) % SIDE][:, near_step, far_step] for spot in range(SIDE)],
                    axis=2,
                )
                for far_step in range(SIDE)
            ]
        )

    held = message(terms, 0)
    for shift in (1, 3, 2):
        held = held + shift_by(message(sent, shift - 1), shift, 0).astype(F32)
    netted = held[0]
    for shift in (1, 3, 2):
        half = (held[shift] * 0.5).astype(jnp.float16)
        netted = netted + shift_by(half, shift, 1).astype(F32) * 2.0

    positive = jnp.maximum(netted, 0.0).reshape(STEPS * OWN, SIDE * CHUNK)
    pick = (jnp.arange(SIDE * CHUNK)[:, None] % REPL == jnp.arange(REPL)[None, :]).astype(F32)
    sums = jnp.dot(positive, pick, precision=lax.Precision.HIGHEST).reshape(STEPS, 2, SPD, REPL)
    kept = lax.dynamic_index_in_dim(sums, core, 1, keepdims=False)
    given = lax.dynamic_index_in_dim(sums, 1 - core, 1, keepdims=False)
    sums = kept + swap_core(given)
    total = sums
    for shift in (1, 3, 2):
        total = total + lax.ppermute(
            sums, "rep", [(i, (i + shift) % SIDE) for i in range(SIDE)]
        )
    per_replicate = total * (1.0 / PATHS)
    exposure = jnp.mean(per_replicate, axis=2)
    deviation = per_replicate - exposure[:, :, None]
    spread = jnp.sqrt(
        PATHS * jnp.sum(deviation * deviation, axis=2) / ((REPL - 1) * REPL)
    )
    return (exposure, spread)


def solution(mesh):
    return jax.shard_map(
        body,
        mesh=mesh,
        in_specs=(
            P(None, ("rep", "set"), None),
            P(),
            P(None, None, "set", None),
            P(None, "set", None),
            P("set"),
            P("set"),
        ),
        out_specs=(P(None, "set"), P(None, "set")),
        check_vma=False,
    )
```

```python
import jax
import jax.numpy as jnp
from jax import lax
from jax.experimental import pallas as pl
from jax.experimental.pallas import tpu as pltpu
from jax.sharding import PartitionSpec as P

STEPS = 3
PATHS = 1024
REPL = 8
SPD = 4
SIDE = 4
BPD = 32
TB = 64
BASIS = 256
FACTORS = 20000
FACTOR_TILE = 6784
ROWS = 64
CHUNK = SIDE * ROWS
OWN = 2 * SPD
GROUP = 4
ORDER = ((3,), (2, 1))
F32 = jnp.float32
BF16 = jnp.bfloat16


def ring_pairs(shift, stage):
    pairs = []
    for z in range(SIDE):
        for x in range(SIDE):
            for core in range(2):
                if (core + stage) % 2 == 0:
                    to = (z, (x + shift) % SIDE, core)
                else:
                    to = ((z + shift) % SIDE, x, core)
                pairs.append((z * 8 + x * 2 + core, to[0] * 8 + to[1] * 2 + to[2]))
    return pairs


CORE_PAIRS = [(i, i ^ 1) for i in range(2 * SIDE * SIDE)]


def shift_by(value, shift, stage):
    return lax.ppermute(value, "set", ring_pairs(shift, stage))


def swap_core(value):
    return lax.ppermute(value, "set", CORE_PAIRS)


def dot(a, b, dims):
    return lax.dot_general(a, b, (dims, ((), ())), preferred_element_type=F32)


def net_rows(live_ref, rows_ref, weights, floor_ref, hot_ref, out_ref, sums_ref, copies=None):
    trade = lax.broadcasted_iota(jnp.int32, (TB, CHUNK), 0)
    for step in range(STEPS):
        rows = rows_ref[:, step].reshape(CHUNK, BASIS)
        for half in range(2):
            if copies and half == 0:
                copies[step].wait()
            for first in range(0, BPD, GROUP):
                trades = slice(first * TB, (first + GROUP) * TB)
                values = dot(weights[half][step, trades, :], rows, ((1,), (1,)))
                for block in range(GROUP):
                    spot = half * BPD + first + block
                    floor = floor_ref[step, half, :, first + block : first + block + 1]
                    value = jnp.maximum(values[block * TB : (block + 1) * TB], floor)
                    value = jnp.where(trade < live_ref[spot], value, 0.0)
                    sums = value[:8]
                    for part in range(8, TB, 8):
                        sums = sums + value[part : part + 8]
                    sums_ref[spot * 8 : spot * 8 + 8, :] = sums
        sums = sums_ref[...]
        high = sums.astype(BF16)
        low = (sums - high.astype(F32)).astype(BF16)
        hot = hot_ref[...]
        out_ref[step] = dot(hot, high, ((1,), (0,))) + dot(hot, low, ((1,), (0,)))


def net_first_kernel(
    live_ref,
    rows_ref,
    mine_ref,
    other_ref,
    my_floor_ref,
    other_floor_ref,
    hot_ref,
    out_ref,
    held_ref,
    floor_ref,
    sums_ref,
    sems,
):
    copies = [
        pltpu.make_async_copy(mine_ref.at[step], held_ref.at[step], sems.at[step])
        for step in range(STEPS)
    ]
    for copy in copies:
        copy.start()
    for step in range(STEPS):
        floor_ref[step, 0] = jnp.transpose(my_floor_ref[step])
        floor_ref[step, 1] = jnp.transpose(other_floor_ref[step])
    weights = (held_ref, other_ref)
    net_rows(live_ref, rows_ref, weights, floor_ref, hot_ref, out_ref, sums_ref, copies)


def net_next_kernel(live_ref, held_ref, other_ref, floor_ref, hot_ref, *refs):
    count = len(refs) // 2
    weights = (held_ref, other_ref)
    for rows_ref, out_ref in zip(refs[:count], refs[count:-1]):
        net_rows(live_ref, rows_ref, weights, floor_ref, hot_ref, out_ref, refs[-1])


VMEM = pl.BlockSpec(memory_space=pltpu.VMEM)
SMEM = pl.BlockSpec(memory_space=pltpu.SMEM)
HBM = pl.BlockSpec(memory_space=pltpu.HBM)


TERMS = (STEPS, SIDE * SIDE * OWN, CHUNK)
HELD = (STEPS, BPD * TB, BASIS)


def net_first(rows, live, mine, other, my_floors, other_floors, hot):
    mine = pltpu.with_memory_space_constraint(mine, pltpu.HBM)
    other = pltpu.with_memory_space_constraint(other, pltpu.VMEM)
    return pl.pallas_call(
        net_first_kernel,
        in_specs=[SMEM, VMEM, HBM, VMEM, VMEM, VMEM, VMEM],
        out_specs=(VMEM, VMEM, VMEM),
        out_shape=(
            jax.ShapeDtypeStruct(TERMS, F32),
            pltpu.VMEM(HELD, BF16),
            jax.ShapeDtypeStruct((STEPS, 2, TB, BPD), F32),
        ),
        scratch_shapes=[
            pltpu.VMEM((2 * BPD * 8, CHUNK), F32),
            pltpu.SemaphoreType.DMA((STEPS,)),
        ],
        compiler_params=pltpu.CompilerParams(vmem_limit_bytes=12 << 20),
        name="net_first",
    )(live, rows, mine, other, my_floors, other_floors, hot)


def net_next(chunks, live, held, other, floors, hot):
    held = pltpu.with_memory_space_constraint(held, pltpu.VMEM)
    other = pltpu.with_memory_space_constraint(other, pltpu.VMEM)
    return pl.pallas_call(
        net_next_kernel,
        in_specs=[SMEM] + [VMEM] * (4 + len(chunks)),
        out_specs=[VMEM] * len(chunks),
        out_shape=[jax.ShapeDtypeStruct(TERMS, F32)] * len(chunks),
        scratch_shapes=[pltpu.VMEM((2 * BPD * 8, CHUNK), F32)],
        compiler_params=pltpu.CompilerParams(vmem_limit_bytes=12 << 20),
        name="net_next",
    )(live, held, other, floors, hot, *chunks)


def basis_kernel(scenarios_ref, projection_ref, out_ref, sums_ref):
    step = pl.program_id(0)
    last = pl.num_programs(0) - 1
    width = FACTORS - (-(-FACTORS // FACTOR_TILE) - 1) * FACTOR_TILE
    rows = STEPS * ROWS

    @pl.when(step == 0)
    def _():
        sums_ref[...] = jnp.zeros_like(sums_ref)

    @pl.when(step < last)
    def _():
        tile = scenarios_ref[...].reshape(rows, FACTOR_TILE)
        sums_ref[...] += dot(tile, projection_ref[...], ((1,), (0,)))

    @pl.when(step == last)
    def _():
        tile = scenarios_ref[:, :, :width].reshape(rows, width)
        sums = sums_ref[...] + dot(tile, projection_ref[:width, :], ((1,), (0,)))
        out_ref[...] = jnp.tanh(sums).astype(BF16).reshape(STEPS, ROWS, BASIS)


def make_basis(scenarios, projection):
    scenarios = pltpu.with_memory_space_constraint(scenarios, pltpu.HBM)
    projection = pltpu.with_memory_space_constraint(projection, pltpu.HBM)
    return pl.pallas_call(
        basis_kernel,
        grid=(-(-FACTORS // FACTOR_TILE),),
        in_specs=[
            pl.BlockSpec((STEPS, ROWS, FACTOR_TILE), lambda k: (0, 0, k)),
            pl.BlockSpec((FACTOR_TILE, BASIS), lambda k: (k, 0)),
        ],
        out_specs=pl.BlockSpec((STEPS, ROWS, BASIS), lambda k: (0, 0, 0)),
        out_shape=jax.ShapeDtypeStruct((STEPS, ROWS, BASIS), BF16),
        scratch_shapes=[pltpu.VMEM((STEPS * ROWS, BASIS), F32)],
        compiler_params=pltpu.CompilerParams(vmem_limit_bytes=24 << 20),
        name="basis",
    )(scenarios, projection)


def line_kernel(first_ref, *refs):
    out_ref = refs[-1]
    for step in range(SIDE):
        out_ref[lax.rem(first_ref[0] + step, SIDE)] = refs[step][...]


def make_line(first, parts):
    return pl.pallas_call(
        line_kernel,
        in_specs=[SMEM] + [pl.BlockSpec()] * SIDE,
        out_specs=pl.BlockSpec(),
        out_shape=jax.ShapeDtypeStruct((SIDE, STEPS, ROWS, BASIS), BF16),
        compiler_params=pltpu.CompilerParams(vmem_limit_bytes=4 << 20),
        name="line",
    )(first.reshape(1), *parts)


def body(scenarios, projection, coefs, exercise, block_set, block_live):
    place = lax.axis_index("set")
    z, x, core = place // 8, (place // 2) % SIDE, place % 2

    basis = make_basis(scenarios, projection)
    weights = jnp.transpose(coefs, (0, 2, 3, 1)).reshape(STEPS, BPD * TB, BASIS)

    first = jnp.where(core == 0, x, z)
    line = make_line(first, [basis] + [shift_by(basis, shift, 0) for shift in (3, 2, 1)])

    other_weights = swap_core(weights)
    exercise, line = lax.optimization_barrier((exercise, line))
    other_floors = swap_core(exercise)
    blocks = jnp.stack([block_set, block_live])
    blocks = jnp.concatenate([blocks, swap_core(blocks)], axis=1)

    near = (first + jnp.arange(SIDE)) % SIDE
    second = jnp.where(core == 0, z, x)
    far = (second + jnp.arange(SIDE)) % SIDE
    chip = jnp.where(
        core == 0, far[None, :] * SIDE + near[:, None], near[:, None] * SIDE + far[None, :]
    )
    ids = (chip[:, :, None] * OWN + jnp.arange(OWN)).reshape(-1)
    owners = jnp.repeat(blocks[0], 8)
    hot = (ids[:, None] == owners[None, :]).astype(BF16)

    arrived = {shift: shift_by(line, shift, 1) for shift in (1, 3, 2)}
    terms, sent = {}, {}

    def keep(shifts, results):
        for shift, term in zip(shifts, results):
            terms[shift] = term.reshape(STEPS, SIDE, SIDE, OWN, CHUNK)
            sent[shift] = terms[shift][:, 1:].astype(jnp.float16)

    term, held, floors = net_first(
        line, blocks[1], weights, other_weights, exercise, other_floors, hot
    )
    keep((0,), (term,))
    last = 0
    for shifts in ORDER:
        chunks, sent[last] = lax.optimization_barrier(
            ([arrived[shift] for shift in shifts], sent[last])
        )
        keep(shifts, net_next(chunks, blocks[1], held, other_weights, floors, hot))
        last = shifts[-1]

    def message(values, near_step):
        return jnp.stack(
            [
                jnp.concatenate(
                    [values[(spot - far_step) % SIDE][:, near_step, far_step] for spot in range(SIDE)],
                    axis=2,
                )
                for far_step in range(SIDE)
            ]
        )

    held = message(terms, 0)
    for shift in (1, 3, 2):
        held = held + shift_by(message(sent, shift - 1), shift, 0).astype(F32)
    netted = held[0]
    for shift in (1, 3, 2):
        half = (held[shift] * 0.5).astype(jnp.float16)
        netted = netted + shift_by(half, shift, 1).astype(F32) * 2.0

    positive = jnp.maximum(netted, 0.0).reshape(STEPS * OWN, SIDE * CHUNK)
    pick = (jnp.arange(SIDE * CHUNK)[:, None] % REPL == jnp.arange(REPL)[None, :]).astype(F32)
    sums = jnp.dot(positive, pick, precision=lax.Precision.HIGHEST).reshape(STEPS, 2, SPD, REPL)
    kept = lax.dynamic_index_in_dim(sums, core, 1, keepdims=False)
    given = lax.dynamic_index_in_dim(sums, 1 - core, 1, keepdims=False)
    sums = kept + swap_core(given)
    total = sums
    for shift in (1, 3, 2):
        total = total + lax.ppermute(
            sums, "rep", [(i, (i + shift) % SIDE) for i in range(SIDE)]
        )
    per_replicate = total * (1.0 / PATHS)
    exposure = jnp.mean(per_replicate, axis=2)
    deviation = per_replicate - exposure[:, :, None]
    spread = jnp.sqrt(
        PATHS * jnp.sum(deviation * deviation, axis=2) / ((REPL - 1) * REPL)
    )
    return (exposure, spread)


def solution(mesh):
    return jax.shard_map(
        body,
        mesh=mesh,
        in_specs=(
            P(None, ("rep", "set"), None),
            P(),
            P(None, None, "set", None),
            P(None, "set", None),
            P("set"),
            P("set"),
        ),
        out_specs=(P(None, "set"), P(None, "set")),
        check_vma=False,
    )
```

```python
import jax
import jax.numpy as jnp
from jax import lax
from jax.experimental import pallas as pl
from jax.experimental.pallas import tpu as pltpu
from jax.sharding import PartitionSpec as P

STEPS = 3
PATHS = 1024
REPL = 8
SPD = 4
SIDE = 4
BPD = 32
TB = 64
BASIS = 256
FACTORS = 20000
FACTOR_TILE = 6784
ROWS = 64
CHUNK = SIDE * ROWS
OWN = 2 * SPD
GROUP = 4
ORDER = ((3,), (2, 1))
F32 = jnp.float32
BF16 = jnp.bfloat16


def ring_pairs(shift, stage):
    pairs = []
    for z in range(SIDE):
        for x in range(SIDE):
            for core in range(2):
                if (core + stage) % 2 == 0:
                    to = (z, (x + shift) % SIDE, core)
                else:
                    to = ((z + shift) % SIDE, x, core)
                pairs.append((z * 8 + x * 2 + core, to[0] * 8 + to[1] * 2 + to[2]))
    return pairs


CORE_PAIRS = [(i, i ^ 1) for i in range(2 * SIDE * SIDE)]


def shift_by(value, shift, stage):
    return lax.ppermute(value, "set", ring_pairs(shift, stage))


def swap_core(value):
    return lax.ppermute(value, "set", CORE_PAIRS)


def dot(a, b, dims):
    return lax.dot_general(a, b, (dims, ((), ())), preferred_element_type=F32)


def net_rows(live_ref, rows_ref, weights, floor_ref, hot_ref, out_ref, sums_ref, copies=None):
    trade = lax.broadcasted_iota(jnp.int32, (TB, CHUNK), 0)
    for step in range(STEPS):
        rows = rows_ref[:, step].reshape(CHUNK, BASIS)
        for half in range(2):
            if copies and half == 0:
                copies[step].wait()
            for first in range(0, BPD, GROUP):
                trades = slice(first * TB, (first + GROUP) * TB)
                values = dot(weights[half][step, trades, :], rows, ((1,), (1,)))
                for block in range(GROUP):
                    spot = half * BPD + first + block
                    floor = floor_ref[step, half, :, first + block : first + block + 1]
                    value = jnp.maximum(values[block * TB : (block + 1) * TB], floor)
                    value = jnp.where(trade < live_ref[spot], value, 0.0)
                    sums = value[:8]
                    for part in range(8, TB, 8):
                        sums = sums + value[part : part + 8]
                    sums_ref[spot * 8 : spot * 8 + 8, :] = sums
        sums = sums_ref[...]
        high = sums.astype(BF16)
        low = (sums - high.astype(F32)).astype(BF16)
        hot = hot_ref[...]
        out_ref[step] = dot(hot, high, ((1,), (0,))) + dot(hot, low, ((1,), (0,)))


def net_first_kernel(
    live_ref,
    rows_ref,
    mine_ref,
    other_ref,
    my_floor_ref,
    other_floor_ref,
    hot_ref,
    out_ref,
    held_ref,
    floor_ref,
    sums_ref,
    stage_ref,
    sems,
):
    floor_copy = pltpu.make_async_copy(my_floor_ref, stage_ref, sems.at[STEPS])
    floor_copy.start()
    copies = [
        pltpu.make_async_copy(mine_ref.at[step], held_ref.at[step], sems.at[step])
        for step in range(STEPS)
    ]
    for copy in copies:
        copy.start()
    floor_copy.wait()
    for step in range(STEPS):
        floor_ref[step, 0] = jnp.transpose(stage_ref[step])
        floor_ref[step, 1] = jnp.transpose(other_floor_ref[step])
    weights = (held_ref, other_ref)
    net_rows(live_ref, rows_ref, weights, floor_ref, hot_ref, out_ref, sums_ref, copies)


def net_next_kernel(live_ref, held_ref, other_ref, floor_ref, hot_ref, *refs):
    count = len(refs) // 2
    weights = (held_ref, other_ref)
    for rows_ref, out_ref in zip(refs[:count], refs[count:-1]):
        net_rows(live_ref, rows_ref, weights, floor_ref, hot_ref, out_ref, refs[-1])


VMEM = pl.BlockSpec(memory_space=pltpu.VMEM)
SMEM = pl.BlockSpec(memory_space=pltpu.SMEM)
HBM = pl.BlockSpec(memory_space=pltpu.HBM)


TERMS = (STEPS, SIDE * SIDE * OWN, CHUNK)
HELD = (STEPS, BPD * TB, BASIS)


def net_first(rows, live, mine, other, my_floors, other_floors, hot):
    mine = pltpu.with_memory_space_constraint(mine, pltpu.HBM)
    my_floors = pltpu.with_memory_space_constraint(my_floors, pltpu.HBM)
    other = pltpu.with_memory_space_constraint(other, pltpu.VMEM)
    return pl.pallas_call(
        net_first_kernel,
        in_specs=[SMEM, VMEM, HBM, VMEM, HBM, VMEM, VMEM],
        out_specs=(VMEM, VMEM, VMEM),
        out_shape=(
            jax.ShapeDtypeStruct(TERMS, F32),
            pltpu.VMEM(HELD, BF16),
            jax.ShapeDtypeStruct((STEPS, 2, TB, BPD), F32),
        ),
        scratch_shapes=[
            pltpu.VMEM((2 * BPD * 8, CHUNK), F32),
            pltpu.VMEM((STEPS, BPD, TB), F32),
            pltpu.SemaphoreType.DMA((STEPS + 1,)),
        ],
        compiler_params=pltpu.CompilerParams(vmem_limit_bytes=12 << 20),
        name="net_first",
    )(live, rows, mine, other, my_floors, other_floors, hot)


def net_next(chunks, live, held, other, floors, hot):
    held = pltpu.with_memory_space_constraint(held, pltpu.VMEM)
    other = pltpu.with_memory_space_constraint(other, pltpu.VMEM)
    return pl.pallas_call(
        net_next_kernel,
        in_specs=[SMEM] + [VMEM] * (4 + len(chunks)),
        out_specs=[VMEM] * len(chunks),
        out_shape=[jax.ShapeDtypeStruct(TERMS, F32)] * len(chunks),
        scratch_shapes=[pltpu.VMEM((2 * BPD * 8, CHUNK), F32)],
        compiler_params=pltpu.CompilerParams(vmem_limit_bytes=12 << 20),
        name="net_next",
    )(live, held, other, floors, hot, *chunks)


def basis_kernel(scenarios_ref, projection_ref, out_ref, sums_ref):
    step = pl.program_id(0)
    last = pl.num_programs(0) - 1
    width = FACTORS - (-(-FACTORS // FACTOR_TILE) - 1) * FACTOR_TILE
    rows = STEPS * ROWS

    @pl.when(step == 0)
    def _():
        sums_ref[...] = jnp.zeros_like(sums_ref)

    @pl.when(step < last)
    def _():
        tile = scenarios_ref[...].reshape(rows, FACTOR_TILE)
        sums_ref[...] += dot(tile, projection_ref[...], ((1,), (0,)))

    @pl.when(step == last)
    def _():
        tile = scenarios_ref[:, :, :width].reshape(rows, width)
        sums = sums_ref[...] + dot(tile, projection_ref[:width, :], ((1,), (0,)))
        out_ref[...] = jnp.tanh(sums).astype(BF16).reshape(STEPS, ROWS, BASIS)


def make_basis(scenarios, projection):
    scenarios = pltpu.with_memory_space_constraint(scenarios, pltpu.HBM)
    projection = pltpu.with_memory_space_constraint(projection, pltpu.HBM)
    return pl.pallas_call(
        basis_kernel,
        grid=(-(-FACTORS // FACTOR_TILE),),
        in_specs=[
            pl.BlockSpec((STEPS, ROWS, FACTOR_TILE), lambda k: (0, 0, k)),
            pl.BlockSpec((FACTOR_TILE, BASIS), lambda k: (k, 0)),
        ],
        out_specs=pl.BlockSpec((STEPS, ROWS, BASIS), lambda k: (0, 0, 0)),
        out_shape=jax.ShapeDtypeStruct((STEPS, ROWS, BASIS), BF16),
        scratch_shapes=[pltpu.VMEM((STEPS * ROWS, BASIS), F32)],
        compiler_params=pltpu.CompilerParams(vmem_limit_bytes=24 << 20),
        name="basis",
    )(scenarios, projection)


def line_kernel(first_ref, *refs):
    out_ref = refs[-1]
    for step in range(SIDE):
        out_ref[lax.rem(first_ref[0] + step, SIDE)] = refs[step][...]


def make_line(first, parts):
    return pl.pallas_call(
        line_kernel,
        in_specs=[SMEM] + [pl.BlockSpec()] * SIDE,
        out_specs=pl.BlockSpec(),
        out_shape=jax.ShapeDtypeStruct((SIDE, STEPS, ROWS, BASIS), BF16),
        compiler_params=pltpu.CompilerParams(vmem_limit_bytes=4 << 20),
        name="line",
    )(first.reshape(1), *parts)


def body(scenarios, projection, coefs, exercise, block_set, block_live):
    place = lax.axis_index("set")
    z, x, core = place // 8, (place // 2) % SIDE, place % 2

    basis = make_basis(scenarios, projection)
    weights = jnp.transpose(coefs, (0, 2, 3, 1)).reshape(STEPS, BPD * TB, BASIS)

    first = jnp.where(core == 0, x, z)
    line = make_line(first, [basis] + [shift_by(basis, shift, 0) for shift in (3, 2, 1)])

    other_weights = swap_core(weights)
    sent_floors, line = lax.optimization_barrier((exercise, line))
    other_floors = swap_core(sent_floors)
    blocks = jnp.stack([block_set, block_live])
    blocks = jnp.concatenate([blocks, swap_core(blocks)], axis=1)

    near = (first + jnp.arange(SIDE)) % SIDE
    second = jnp.where(core == 0, z, x)
    far = (second + jnp.arange(SIDE)) % SIDE
    chip = jnp.where(
        core == 0, far[None, :] * SIDE + near[:, None], near[:, None] * SIDE + far[None, :]
    )
    ids = (chip[:, :, None] * OWN + jnp.arange(OWN)).reshape(-1)
    owners = jnp.repeat(blocks[0], 8)
    hot = (ids[:, None] == owners[None, :]).astype(BF16)

    arrived = {shift: shift_by(line, shift, 1) for shift in (1, 3, 2)}
    terms, sent = {}, {}

    def keep(shifts, results):
        for shift, term in zip(shifts, results):
            terms[shift] = term.reshape(STEPS, SIDE, SIDE, OWN, CHUNK)
            sent[shift] = terms[shift][:, 1:].astype(jnp.float16)

    term, held, floors = net_first(
        line, blocks[1], weights, other_weights, exercise, other_floors, hot
    )
    keep((0,), (term,))
    last = 0
    for shifts in ORDER:
        chunks, sent[last] = lax.optimization_barrier(
            ([arrived[shift] for shift in shifts], sent[last])
        )
        keep(shifts, net_next(chunks, blocks[1], held, other_weights, floors, hot))
        last = shifts[-1]

    def message(values, near_step):
        return jnp.stack(
            [
                jnp.concatenate(
                    [values[(spot - far_step) % SIDE][:, near_step, far_step] for spot in range(SIDE)],
                    axis=2,
                )
                for far_step in range(SIDE)
            ]
        )

    held = message(terms, 0)
    for shift in (2, 3, 1):
        held = held + shift_by(message(sent, shift - 1), shift, 0).astype(F32)
    netted = held[0]
    for shift in (2, 3, 1):
        half = (held[shift] * 0.5).astype(jnp.float16)
        netted = netted + shift_by(half, shift, 1).astype(F32) * 2.0

    positive = jnp.maximum(netted, 0.0).reshape(STEPS * OWN, SIDE * CHUNK)
    pick = (jnp.arange(SIDE * CHUNK)[:, None] % REPL == jnp.arange(REPL)[None, :]).astype(F32)
    sums = jnp.dot(positive, pick, precision=lax.Precision.HIGHEST).reshape(STEPS, 2, SPD, REPL)
    kept = lax.dynamic_index_in_dim(sums, core, 1, keepdims=False)
    given = lax.dynamic_index_in_dim(sums, 1 - core, 1, keepdims=False)
    sums = kept + swap_core(given)
    total = sums
    for shift in (2, 3, 1):
        total = total + lax.ppermute(
            sums, "rep", [(i, (i + shift) % SIDE) for i in range(SIDE)]
        )
    per_replicate = total * (1.0 / PATHS)
    exposure = jnp.mean(per_replicate, axis=2)
    deviation = per_replicate - exposure[:, :, None]
    spread = jnp.sqrt(
        PATHS * jnp.sum(deviation * deviation, axis=2) / ((REPL - 1) * REPL)
    )
    return (exposure, spread)


def solution(mesh):
    return jax.shard_map(
        body,
        mesh=mesh,
        in_specs=(
            P(None, ("rep", "set"), None),
            P(),
            P(None, None, "set", None),
            P(None, "set", None),
            P("set"),
            P("set"),
        ),
        out_specs=(P(None, "set"), P(None, "set")),
        check_vma=False,
    )
```

```python
import jax
import jax.numpy as jnp
from jax import lax
from jax.experimental import pallas as pl
from jax.experimental.pallas import tpu as pltpu
from jax.sharding import PartitionSpec as P

STEPS = 3
PATHS = 1024
REPL = 8
SPD = 4
SIDE = 4
BPD = 32
TB = 64
BASIS = 256
FACTORS = 20000
FACTOR_TILE = 6784
ROWS = 64
CHUNK = SIDE * ROWS
OWN = 2 * SPD
GROUP = 4
ORDER = ((1,), (3, 2))
F32 = jnp.float32
BF16 = jnp.bfloat16


def ring_pairs(shift, stage):
    pairs = []
    for z in range(SIDE):
        for x in range(SIDE):
            for core in range(2):
                if (core + stage) % 2 == 0:
                    to = (z, (x + shift) % SIDE, core)
                else:
                    to = ((z + shift) % SIDE, x, core)
                pairs.append((z * 8 + x * 2 + core, to[0] * 8 + to[1] * 2 + to[2]))
    return pairs


CORE_PAIRS = [(i, i ^ 1) for i in range(2 * SIDE * SIDE)]


def shift_by(value, shift, stage):
    return lax.ppermute(value, "set", ring_pairs(shift, stage))


def swap_core(value):
    return lax.ppermute(value, "set", CORE_PAIRS)


def dot(a, b, dims):
    return lax.dot_general(a, b, (dims, ((), ())), preferred_element_type=F32)


def net_rows(live_ref, rows_ref, weights, floor_ref, hot_ref, out_ref, sums_ref, copies=None):
    trade = lax.broadcasted_iota(jnp.int32, (TB, CHUNK), 0)
    for step in range(STEPS):
        rows = rows_ref[:, step].reshape(CHUNK, BASIS)
        for half in range(2):
            if copies and half == 0:
                copies[step].wait()
            for first in range(0, BPD, GROUP):
                trades = slice(first * TB, (first + GROUP) * TB)
                values = dot(weights[half][step, trades, :], rows, ((1,), (1,)))
                for block in range(GROUP):
                    spot = half * BPD + first + block
                    floor = floor_ref[step, half, :, first + block : first + block + 1]
                    value = jnp.maximum(values[block * TB : (block + 1) * TB], floor)
                    value = jnp.where(trade < live_ref[spot], value, 0.0)
                    sums = value[:8]
                    for part in range(8, TB, 8):
                        sums = sums + value[part : part + 8]
                    sums_ref[spot * 8 : spot * 8 + 8, :] = sums
        sums = sums_ref[...]
        high = sums.astype(BF16)
        low = (sums - high.astype(F32)).astype(BF16)
        hot = hot_ref[...]
        out_ref[step] = dot(hot, high, ((1,), (0,))) + dot(hot, low, ((1,), (0,)))


def net_first_kernel(
    live_ref,
    rows_ref,
    mine_ref,
    other_ref,
    my_floor_ref,
    other_floor_ref,
    hot_ref,
    out_ref,
    held_ref,
    floor_ref,
    sums_ref,
    stage_ref,
    sems,
):
    floor_copy = pltpu.make_async_copy(my_floor_ref, stage_ref, sems.at[STEPS])
    floor_copy.start()
    copies = [
        pltpu.make_async_copy(mine_ref.at[step], held_ref.at[step], sems.at[step])
        for step in range(STEPS)
    ]
    for copy in copies:
        copy.start()
    floor_copy.wait()
    for step in range(STEPS):
        floor_ref[step, 0] = jnp.transpose(stage_ref[step])
        floor_ref[step, 1] = jnp.transpose(other_floor_ref[step])
    weights = (held_ref, other_ref)
    net_rows(live_ref, rows_ref, weights, floor_ref, hot_ref, out_ref, sums_ref, copies)


def net_next_kernel(live_ref, held_ref, other_ref, floor_ref, hot_ref, *refs):
    count = len(refs) // 2
    weights = (held_ref, other_ref)
    for rows_ref, out_ref in zip(refs[:count], refs[count:-1]):
        net_rows(live_ref, rows_ref, weights, floor_ref, hot_ref, out_ref, refs[-1])


VMEM = pl.BlockSpec(memory_space=pltpu.VMEM)
SMEM = pl.BlockSpec(memory_space=pltpu.SMEM)
HBM = pl.BlockSpec(memory_space=pltpu.HBM)


TERMS = (STEPS, SIDE * SIDE * OWN, CHUNK)
HELD = (STEPS, BPD * TB, BASIS)


def net_first(rows, live, mine, other, my_floors, other_floors, hot):
    mine = pltpu.with_memory_space_constraint(mine, pltpu.HBM)
    my_floors = pltpu.with_memory_space_constraint(my_floors, pltpu.HBM)
    other = pltpu.with_memory_space_constraint(other, pltpu.VMEM)
    return pl.pallas_call(
        net_first_kernel,
        in_specs=[SMEM, VMEM, HBM, VMEM, HBM, VMEM, VMEM],
        out_specs=(VMEM, VMEM, VMEM),
        out_shape=(
            jax.ShapeDtypeStruct(TERMS, F32),
            pltpu.VMEM(HELD, BF16),
            jax.ShapeDtypeStruct((STEPS, 2, TB, BPD), F32),
        ),
        scratch_shapes=[
            pltpu.VMEM((2 * BPD * 8, CHUNK), F32),
            pltpu.VMEM((STEPS, BPD, TB), F32),
            pltpu.SemaphoreType.DMA((STEPS + 1,)),
        ],
        compiler_params=pltpu.CompilerParams(vmem_limit_bytes=12 << 20),
        name="net_first",
    )(live, rows, mine, other, my_floors, other_floors, hot)


def net_next(chunks, live, held, other, floors, hot):
    held = pltpu.with_memory_space_constraint(held, pltpu.VMEM)
    other = pltpu.with_memory_space_constraint(other, pltpu.VMEM)
    return pl.pallas_call(
        net_next_kernel,
        in_specs=[SMEM] + [VMEM] * (4 + len(chunks)),
        out_specs=[VMEM] * len(chunks),
        out_shape=[jax.ShapeDtypeStruct(TERMS, F32)] * len(chunks),
        scratch_shapes=[pltpu.VMEM((2 * BPD * 8, CHUNK), F32)],
        compiler_params=pltpu.CompilerParams(vmem_limit_bytes=12 << 20),
        name="net_next",
    )(live, held, other, floors, hot, *chunks)


def basis_kernel(scenarios_ref, projection_ref, out_ref, sums_ref):
    step = pl.program_id(0)
    last = pl.num_programs(0) - 1
    width = FACTORS - (-(-FACTORS // FACTOR_TILE) - 1) * FACTOR_TILE
    rows = STEPS * ROWS

    @pl.when(step == 0)
    def _():
        sums_ref[...] = jnp.zeros_like(sums_ref)

    @pl.when(step < last)
    def _():
        tile = scenarios_ref[...].reshape(rows, FACTOR_TILE)
        sums_ref[...] += dot(tile, projection_ref[...], ((1,), (0,)))

    @pl.when(step == last)
    def _():
        tile = scenarios_ref[:, :, :width].reshape(rows, width)
        sums = sums_ref[...] + dot(tile, projection_ref[:width, :], ((1,), (0,)))
        out_ref[...] = jnp.tanh(sums).astype(BF16).reshape(STEPS, ROWS, BASIS)


def make_basis(scenarios, projection):
    scenarios = pltpu.with_memory_space_constraint(scenarios, pltpu.HBM)
    projection = pltpu.with_memory_space_constraint(projection, pltpu.HBM)
    return pl.pallas_call(
        basis_kernel,
        grid=(-(-FACTORS // FACTOR_TILE),),
        in_specs=[
            pl.BlockSpec((STEPS, ROWS, FACTOR_TILE), lambda k: (0, 0, k)),
            pl.BlockSpec((FACTOR_TILE, BASIS), lambda k: (k, 0)),
        ],
        out_specs=pl.BlockSpec((STEPS, ROWS, BASIS), lambda k: (0, 0, 0)),
        out_shape=jax.ShapeDtypeStruct((STEPS, ROWS, BASIS), BF16),
        scratch_shapes=[pltpu.VMEM((STEPS * ROWS, BASIS), F32)],
        compiler_params=pltpu.CompilerParams(vmem_limit_bytes=24 << 20),
        name="basis",
    )(scenarios, projection)


def line_kernel(first_ref, *refs):
    out_ref = refs[-1]
    for step in range(SIDE):
        out_ref[lax.rem(first_ref[0] + step, SIDE)] = refs[step][...]


def make_line(first, parts):
    return pl.pallas_call(
        line_kernel,
        in_specs=[SMEM] + [pl.BlockSpec()] * SIDE,
        out_specs=pl.BlockSpec(),
        out_shape=jax.ShapeDtypeStruct((SIDE, STEPS, ROWS, BASIS), BF16),
        compiler_params=pltpu.CompilerParams(vmem_limit_bytes=4 << 20),
        name="line",
    )(first.reshape(1), *parts)


def body(scenarios, projection, coefs, exercise, block_set, block_live):
    place = lax.axis_index("set")
    z, x, core = place // 8, (place // 2) % SIDE, place % 2

    basis = make_basis(scenarios, projection)
    weights = jnp.transpose(coefs, (0, 2, 3, 1)).reshape(STEPS, BPD * TB, BASIS)

    first = jnp.where(core == 0, x, z)
    line = make_line(first, [basis] + [shift_by(basis, shift, 0) for shift in (3, 2, 1)])

    other_weights = swap_core(weights)
    sent_floors, line = lax.optimization_barrier((exercise, line))
    other_floors = swap_core(sent_floors)
    blocks = jnp.stack([block_set, block_live])
    blocks = jnp.concatenate([blocks, swap_core(blocks)], axis=1)

    near = (first + jnp.arange(SIDE)) % SIDE
    second = jnp.where(core == 0, z, x)
    far = (second + jnp.arange(SIDE)) % SIDE
    chip = jnp.where(
        core == 0, far[None, :] * SIDE + near[:, None], near[:, None] * SIDE + far[None, :]
    )
    ids = (chip[:, :, None] * OWN + jnp.arange(OWN)).reshape(-1)
    owners = jnp.repeat(blocks[0], 8)
    hot = (ids[:, None] == owners[None, :]).astype(BF16)

    arrived = {shift: shift_by(line, shift, 1) for shift in (1, 3, 2)}
    terms, sent = {}, {}

    def keep(shifts, results):
        for shift, term in zip(shifts, results):
            terms[shift] = term.reshape(STEPS, SIDE, SIDE, OWN, CHUNK)
            sent[shift] = terms[shift][:, 1:].astype(jnp.float16)

    term, held, floors = net_first(
        line, blocks[1], weights, other_weights, exercise, other_floors, hot
    )
    keep((0,), (term,))
    last = 0
    for shifts in ORDER:
        chunks, sent[last] = lax.optimization_barrier(
            ([arrived[shift] for shift in shifts], sent[last])
        )
        keep(shifts, net_next(chunks, blocks[1], held, other_weights, floors, hot))
        last = shifts[-1]

    def message(values, near_step):
        return jnp.stack(
            [
                jnp.concatenate(
                    [values[(spot - far_step) % SIDE][:, near_step, far_step] for spot in range(SIDE)],
                    axis=2,
                )
                for far_step in range(SIDE)
            ]
        )

    held = message(terms, 0)
    for shift in (2, 3, 1):
        held = held + shift_by(message(sent, shift - 1), shift, 0).astype(F32)
    netted = held[0]
    for shift in (2, 3, 1):
        half = (held[shift] * 0.5).astype(jnp.float16)
        netted = netted + shift_by(half, shift, 1).astype(F32) * 2.0

    positive = jnp.maximum(netted, 0.0).reshape(STEPS * OWN, SIDE * CHUNK)
    pick = (jnp.arange(SIDE * CHUNK)[:, None] % REPL == jnp.arange(REPL)[None, :]).astype(F32)
    sums = jnp.dot(positive, pick, precision=lax.Precision.HIGHEST).reshape(STEPS, 2, SPD, REPL)
    kept = lax.dynamic_index_in_dim(sums, core, 1, keepdims=False)
    given = lax.dynamic_index_in_dim(sums, 1 - core, 1, keepdims=False)
    sums = kept + swap_core(given)
    total = sums
    for shift in (2, 3, 1):
        total = total + lax.ppermute(
            sums, "rep", [(i, (i + shift) % SIDE) for i in range(SIDE)]
        )
    per_replicate = total * (1.0 / PATHS)
    exposure = jnp.mean(per_replicate, axis=2)
    deviation = per_replicate - exposure[:, :, None]
    spread = jnp.sqrt(
        PATHS * jnp.sum(deviation * deviation, axis=2) / ((REPL - 1) * REPL)
    )
    return (exposure, spread)


def solution(mesh):
    return jax.shard_map(
        body,
        mesh=mesh,
        in_specs=(
            P(None, ("rep", "set"), None),
            P(),
            P(None, None, "set", None),
            P(None, "set", None),
            P("set"),
            P("set"),
        ),
        out_specs=(P(None, "set"), P(None, "set")),
        check_vma=False,
    )
```
